32 devices in a mesh: wide: 8 (over z, y), narrow: 4 (over x, core).
Axes of the slice: x: 2, y: 2, z: 4, core: 2. Of those that a mesh axis runs over, the one named last changes fastest.
Arguments:
- amplitudes: bfloat16 [256, 32768], P(('wide', 'narrow')), may hold values from -6 to 6
- integrals: bfloat16 [32768, 1024], P('wide', 'narrow'), may hold values from -0.0625 to 0.0625
- block_irrep: int32 [64], replicated, may hold values from 0 to 3
- block_units: int32 [64], replicated, may hold values from 1 to 32, 512 in all
- window_pairs: int32 [1024], replicated, may hold values from 0 to 32767
- panel_owner: int32 [4], replicated, may hold values from 0 to 3, each once
Outputs:
- ladder: bfloat16 [256, 1024], P(('wide', 'narrow'))
The draws below stay inside these ranges and needn't reach their ends.
Inputs may be any that keep to these rules, and one draw needn't show every extreme that they name: `block_units`: the entries sum to 512; one block has exactly 32 units. `panel_owner`: each index of narrow appears once.
All inputs are finite; a program needn't handle non-finite values.
Results may differ from the reference program's by a relative error of at most 0.0017.
Values may be sent and summed in bfloat16 or wider, within the bound.
No kernel may reach another device: no remote copies, remote signals or barrier semaphores. Data moves between devices by JAX's collectives and lax.ppermute only.
A program may use at most 128 MiB of HBM per device.

```python
import math
import jax
import jax.numpy as jnp
import numpy as np
from jax import lax

CD_DEV = 4096
ABP = 256
UNIT = 64
NBLK = 64
NIRREP = 4
VP = 32768
OP = 256
AB = 1024
UNITS = 512
MOSTU = 32
N_WIDE = 8
N_NARROW = 4


def plant(drawn, rng, least, high):
    index_at = [jax.random.randint(jax.random.fold_in(rng, axis), (), 0, length) for axis, length in enumerate(drawn.shape)]
    widest = drawn.shape.index(max(drawn.shape))
    neighbour = index_at[:widest] + [(index_at[widest] + 1) % drawn.shape[widest]] + index_at[widest + 1:]
    return drawn.at[tuple(index_at)].set(least).at[tuple(neighbour)].set(high)


def raised(result, key, source, target, parts, factor):
    owner, partner = [(jnp.arange(result.shape[axis_at]) // (result.shape[axis_at] // parts)).reshape([-1 if axis == axis_at else 1 for axis in range(result.ndim)]) for axis_at in (source, target)]
    chosen = jax.random.permutation(key, parts)[partner]
    strong = (owner == chosen) | (owner == (partner + parts // 2) % parts)
    return jnp.where(strong, factor * result, result)


def block_levels(rng, shape, cuts, low, top_value):
    factor_of, own = 1.0, jax.random.fold_in(rng, 6)
    for position, parts in cuts:
        draws = jnp.exp(jax.random.uniform(jax.random.fold_in(own, position), (parts,), jnp.float32, low / len(cuts), top_value / len(cuts)))
        factor_of = factor_of * jnp.repeat(draws, shape[position] // parts).reshape([-1 if axis == position else 1 for axis in range(len(shape))])
    return factor_of


def profile(number_of, total, reach, skew):
    loads = [(1 << 20) // math.isqrt(grade ** skew) + 1 for grade in range(2, number_of + 1)]
    spare, counts = total - reach - (number_of - 1), [1] * (number_of - 1)
    while spare > 0:
        candidates = [i for i in range(number_of - 1) if counts[i] < reach]
        mass, remaining = sum([loads[i] for i in candidates]), spare
        for i in candidates:
            extra = min(reach - counts[i], max(1, remaining * loads[i] // mass), spare)
            counts[i] = counts[i] + extra
            spare = spare - extra
    return np.array([reach] + counts)


def ragged_sizes(key, amount, total, bound, skew):
    if amount == 2:
        one = jax.random.randint(key, (), max(1, total - bound), min(bound, total - 1) + 1)
        return jnp.stack([one, total - one])
    lengths = jnp.asarray(profile(amount, total, bound, skew), jnp.int32)
    twos = (amount - 1) // 2
    giver, sink = lengths[1:1 + 2 * twos:2], lengths[2:2 + 2 * twos:2]
    margin = jnp.minimum(giver - 1, bound - sink)
    shifted = jax.random.randint(jax.random.fold_in(key, 1), (twos,), 0, 1 << 20) % (margin + 1)
    lengths = lengths.at[1:1 + 2 * twos:2].set(giver - shifted).at[2:2 + 2 * twos:2].set(sink + shifted)
    return lengths[jax.random.permutation(jax.random.fold_in(key, 2), amount)]


def noise(own_key, extent, width, limit, split=(), kind=jnp.bfloat16):
    result = jax.random.normal(own_key, extent, jnp.float32) * width
    if len(split) > 0:
        result = block_levels(own_key, extent, split, -0.22, 0.18) * result
    return jnp.clip(result, min=-limit, max=limit).astype(kind)


def heavy_noise(own_key, extent, scale, most, shards, heavy, held_as=jnp.bfloat16):
    entries = scale * jax.random.normal(own_key, extent, jnp.float32)
    if shards:
        entries = entries * block_levels(own_key, extent, shards, -0.22, 0.18)
    return jnp.clip(raised(entries, jax.random.fold_in(own_key, 3), *heavy), -most, most).astype(held_as)


def setup_inputs(seed: int = 0) -> dict:
    keys = jax.random.split(jax.random.key(seed), 7)
    amplitudes = heavy_noise(keys[0], (OP, VP), 1.0, 6.0, ((0, 32),), (1, 0, 32, 2.75))
    integrals = noise(keys[1], (VP, AB), (VP // 4) ** -0.5, 0.0625, ((0, 8), (1, 4)))
    block_irrep = plant(jax.random.randint(keys[2], (NBLK,), 0, NIRREP), jax.random.fold_in(keys[2], 1), 0, NIRREP - 1).astype(jnp.int32)
    block_units = ragged_sizes(keys[3], NBLK, UNITS, MOSTU, 2).astype(jnp.int32)
    window_pairs = plant(jax.random.randint(keys[4], (AB,), 0, VP), jax.random.fold_in(keys[4], 1), 0, VP - 1).astype(jnp.int32)
    panel_owner = jax.random.permutation(keys[5], N_NARROW).astype(jnp.int32)
    return dict(amplitudes=amplitudes, integrals=integrals, block_irrep=block_irrep, block_units=block_units, window_pairs=window_pairs, panel_owner=panel_owner)


def pair_irreps(window, block_irrep, block_units):
    block_ends = (jnp.cumsum(block_units) * UNIT).astype(jnp.int32)
    block_starts = (block_ends - block_units * UNIT).astype(jnp.int32)
    inside = (window[:, None] >= block_starts[None, :]) & (window[:, None] < block_ends[None, :])
    return jnp.sum(jnp.where(inside, block_irrep[None, :], 0), axis=1).astype(jnp.int32)


def reference(amplitudes, integrals, block_irrep, block_units, window_pairs, panel_owner):
    column_order = (panel_owner[:, None] * ABP + jnp.arange(ABP, dtype=jnp.int32)[None, :]).reshape(-1).astype(jnp.int32)
    out_irrep = pair_irreps(window_pairs[column_order].astype(jnp.int32), block_irrep, block_units)

    def accumulate(accumulated, block_index):
        offset = (block_index * CD_DEV).astype(jnp.int32)
        amp_block = lax.dynamic_slice_in_dim(amplitudes, offset, CD_DEV, 1)
        int_block = lax.dynamic_slice_in_dim(integrals, offset, CD_DEV, 0)[:, column_order]
        contracted = offset + jnp.arange(CD_DEV, dtype=jnp.int32)
        matches = pair_irreps(contracted, block_irrep, block_units)[:, None] == out_irrep[None, :]
        masked = jnp.where(matches, int_block, jnp.zeros_like(int_block))
        return accumulated + jnp.dot(amp_block, masked, preferred_element_type=jnp.float32), None

    accumulated, unused = lax.scan(accumulate, jnp.zeros((OP, AB), jnp.float32), jnp.arange(N_WIDE, dtype=jnp.int32))
    return accumulated.astype(jnp.bfloat16)
```

```python
import jax
import jax.numpy as jnp
from jax import lax
from jax.sharding import PartitionSpec as P

UNIT = 64


def pair_irreps(window, block_irrep, block_units):
    block_ends = jnp.cumsum(block_units) * UNIT
    block_starts = block_ends - block_units * UNIT
    inside = (window[:, None] >= block_starts[None, :]) & (window[:, None] < block_ends[None, :])
    return jnp.sum(jnp.where(inside, block_irrep[None, :], 0), axis=1)


def swap(value, axis, bit):
    size = lax.axis_size(axis)
    return lax.ppermute(value, axis, [(i, i ^ bit) for i in range(size)])


def on_device(amplitudes, integrals, block_irrep, block_units, window_pairs, panel_owner):
    wide, narrow = lax.axis_size("wide"), lax.axis_size("narrow")
    rows = amplitudes.shape[0]
    local_pairs, panel_width = integrals.shape
    me = lax.axis_index("narrow")

    contracted = lax.axis_index("wide") * local_pairs + jnp.arange(local_pairs, dtype=jnp.int32)
    contracted_irrep = pair_irreps(contracted, block_irrep, block_units)
    window = lax.dynamic_slice_in_dim(window_pairs, me * panel_width, panel_width)
    matches = contracted_irrep[:, None] == pair_irreps(window, block_irrep, block_units)[None, :]
    masked = jnp.where(matches, integrals, jnp.zeros_like(integrals))

    own = lax.all_to_all(amplitudes, "wide", split_axis=1, concat_axis=0, tiled=True)
    parts = [own]
    bit = narrow // 2
    offsets = [0]
    while bit:
        parts += [swap(part, "narrow", bit) for part in parts]
        offsets += [offset ^ bit for offset in offsets]
        bit //= 2
    products = jnp.stack(
        [jnp.dot(part, masked, preferred_element_type=jnp.float32) for part in parts]
    )
    slot_of = jnp.asarray(offsets, jnp.int32)
    place = jnp.argsort(slot_of ^ me)
    products = products[place].reshape(narrow, wide, rows, panel_width).swapaxes(0, 1)
    received = lax.all_to_all(
        products.reshape(wide * narrow, rows, panel_width), ("wide", "narrow"), 0, 0
    )
    total = jnp.sum(received.reshape(wide, narrow, rows, panel_width), axis=0)
    ordered = total[panel_owner].astype(jnp.bfloat16)
    return ordered.swapaxes(0, 1).reshape(rows, narrow * panel_width)


def solution(mesh):
    placed = (P(("wide", "narrow"), None), P("wide", "narrow"), P(), P(), P(), P())
    return jax.shard_map(
        on_device,
        mesh=mesh,
        in_specs=placed,
        out_specs=P(("wide", "narrow"), None),
        check_vma=False,
    )
```
